32 devices in a mesh: rack: 4 (over z), dev: 8 (over y, x, core).
Axes of the slice: x: 2, y: 2, z: 4, core: 2. Of those that a mesh axis runs over, the one named last changes fastest.
Arguments:
- span_store: bfloat16 [704, 64, 1024], P(('rack', 'dev')), may hold values from -6 to 6
- helper_offset: int32 [22], replicated, may hold values from 1 to 31, as said below
- plane_index: int32 [64, 16], replicated, may hold values from 0 to 63, as said below
- coupling_pair: int32 [64, 11, 16], P(('rack', 'dev')), may hold values from 0 to 10
- decode_matrix: float32 [64, 4, 11], P(('rack', 'dev')), may hold values from -1.75 to 1.75
- recouple_pair: int32 [64, 64], P(('rack', 'dev')), may hold values from 0 to 63
Outputs:
- rebuilt: bfloat16 [64, 64, 1024], P(('rack', 'dev'))
The draws below stay inside these ranges and needn't reach their ends.
Inputs may be any that keep to these rules, and one draw needn't show every extreme that they name: 22 distinct values; helper slot j of a stripe of device p is always slot j of device p + helper_offset[j] (mod the device count). `plane_index`: each row lists in increasing order the 16 indices z whose base-4 digit number y equals x, for the stripe's lost node (x, y), x below 4 and y below 3.
All inputs are finite; a program needn't handle non-finite values.
Results may differ from the reference program's by a relative error of at most 0.001.
Values may be sent and summed in bfloat16 or wider, within the bound.
No kernel may reach another device: no remote copies, remote signals or barrier semaphores. Data moves between devices by JAX's collectives and lax.ppermute only.
A program may use at most 64 MiB of HBM per device.

```python
import jax
import jax.numpy as jnp
from jax import lax

W = 1024
SUBS = 64
PLANES = 16
HELPERS = 11
GROUP = 4
STORE_DEV = 22
STRIPES = 64
N_RACK = 4
N_DEV = 8


def draw_helper_offset(key, part):
    shuffled = jax.random.permutation(jax.random.fold_in(key, 11), N_RACK * N_DEV - 1)
    return (shuffled[:STORE_DEV] + 1).astype(jnp.int32)


def draw_plane_index(key, part):
    lost_node = jax.random.randint(jax.random.fold_in(key, 23), (STRIPES,), 0, 12)
    digit_value = lost_node % 4
    digit_place = lost_node // 4
    sub_ids = jnp.arange(SUBS, dtype=jnp.int32)
    powers = jnp.where(digit_place == 0, 1, jnp.where(digit_place == 1, 4, 16))
    digits = sub_ids[None, :] // powers[:, None] % 4
    scores = (digits != digit_value[:, None]).astype(jnp.int32) * SUBS + sub_ids[None, :]
    order = jnp.argsort(scores, axis=1, stable=True)
    return order[:, :PLANES].astype(jnp.int32)


def plant(entries, key, smallest, high):
    longest = entries.shape.index(max(entries.shape))
    spots = []
    for shift in (0, 1):
        where = [jax.random.randint(jax.random.fold_in(key, axis), (), 0, length) for axis, length in enumerate(entries.shape)]
        where[longest] = (where[longest] + shift) % entries.shape[longest]
        spots.append(tuple(where))
    return entries.at[spots[0]].set(smallest).at[spots[1]].set(high)


def steps_of(key, dims, split, least, top_value):
    level, own = 1.0, jax.random.fold_in(key, 6)
    for position, parts in split:
        draws = jnp.exp(jax.random.uniform(jax.random.fold_in(own, position), (parts,), jnp.float32, least / len(split), top_value / len(split)))
        level = level * jnp.repeat(draws, dims[position] // parts).reshape([-1 if axis == position else 1 for axis in range(len(dims))])
    return level


def normal_values(stream_key, extent, scale, most, cuts=(), held_as=jnp.bfloat16):
    entries = jax.random.normal(stream_key, extent, jnp.float32) * scale
    if len(cuts) > 0:
        entries = steps_of(stream_key, extent, cuts, -0.22, 0.18) * entries
    return jnp.clip(entries, min=-most, max=most).astype(held_as)


def setup_inputs(seed: int = 0) -> dict:
    streams_of = jax.random.split(jax.random.key(seed), 7)
    span_store = normal_values(streams_of[0], (N_RACK * N_DEV * STORE_DEV, SUBS, W), 1.0, 6.0, ((0, 32),))
    helper_offset = draw_helper_offset(jax.random.fold_in(streams_of[6], 71), 0)
    plane_index = draw_plane_index(jax.random.fold_in(streams_of[6], 71), 0)
    coupling_pair = plant(jax.random.randint(streams_of[3], (STRIPES, HELPERS, PLANES), 0, HELPERS), jax.random.fold_in(streams_of[3], 1), 0, HELPERS - 1).astype(jnp.int32)
    decode_matrix = normal_values(streams_of[4], (STRIPES, GROUP, HELPERS), HELPERS ** -0.5, 1.75, ((0, 32),), jnp.float32)
    recouple_pair = plant(jax.random.randint(streams_of[5], (STRIPES, SUBS), 0, SUBS), jax.random.fold_in(streams_of[5], 1), 0, SUBS - 1).astype(jnp.int32)
    return dict(span_store=span_store, helper_offset=helper_offset, plane_index=plane_index, coupling_pair=coupling_pair, decode_matrix=decode_matrix, recouple_pair=recouple_pair)


COUPLING = 0.6


def repair_stripes(words, decode_block, pair_block, recouple_pairs):
    coded = words.astype(jnp.float32)
    helpers = coded.shape[1]
    helper_ids = jnp.arange(helpers, dtype=jnp.int32)
    choose = (pair_block[..., None] == helper_ids).astype(jnp.float32)
    partner = jnp.einsum("shzg,sgzw->shzw", choose, coded, precision=lax.Precision.HIGHEST)
    coupled_mask = (pair_block != helper_ids[None, :, None]).astype(jnp.float32)
    uncoupled = (coded - COUPLING * coupled_mask[..., None] * partner) / (1.0 - COUPLING * COUPLING)
    decoded = jnp.einsum("sth,shzw->sztw", decode_block, uncoupled, precision=lax.Precision.HIGHEST)
    flat = decoded.reshape(decoded.shape[0], -1, decoded.shape[-1])
    sub_ids = jnp.arange(flat.shape[1], dtype=jnp.int32)
    pick = (recouple_pairs[..., None] == sub_ids).astype(jnp.float32)
    other = jnp.einsum("sab,sbw->saw", pick, flat, precision=lax.Precision.HIGHEST)
    distinct = (recouple_pairs != sub_ids[None, :]).astype(jnp.float32)
    return (flat + COUPLING * distinct[..., None] * other).astype(jnp.bfloat16)


def reference(span_store, helper_offset, plane_index, coupling_pair, decode_matrix, recouple_pair):
    device_count = N_RACK * N_DEV
    slots = helper_offset.shape[0]
    per_device = slots // HELPERS
    columns = span_store.shape[-1]
    stored = span_store.reshape(device_count, slots, SUBS, columns)
    slot_ids = jnp.arange(slots, dtype=jnp.int32)

    def one_primary(primary):
        sources = (primary + helper_offset) % device_count
        stripes = primary * per_device + slot_ids // HELPERS
        planes = plane_index[stripes]
        rows = stored[sources, slot_ids]
        words = rows[slot_ids[:, None], planes].reshape(per_device, HELPERS, PLANES, columns)
        first = (primary * per_device).astype(jnp.int32)
        pairs = lax.dynamic_slice_in_dim(coupling_pair, first, per_device, 0)
        decode_block = lax.dynamic_slice_in_dim(decode_matrix, first, per_device, 0)
        recouple_pairs = lax.dynamic_slice_in_dim(recouple_pair, first, per_device, 0)
        return repair_stripes(words, decode_block, pairs, recouple_pairs)

    rebuilt = lax.map(one_primary, jnp.arange(device_count, dtype=jnp.int32))
    return rebuilt.reshape(device_count * per_device, SUBS, columns)
```

```python
import jax
import jax.numpy as jnp
from jax import lax
from jax.sharding import PartitionSpec as P

COUPLING = 0.6
HIGHEST = lax.Precision.HIGHEST


def repair_matrix(decode_block, pair_block, recouple_pairs, sources, device_count):
    stripes_here, helpers, plane_count = pair_block.shape
    group_size = decode_block.shape[1]
    helper_ids = jnp.arange(helpers, dtype=jnp.int32)
    choose = (pair_block[..., None] == helper_ids).astype(jnp.float32)
    coupled = (pair_block != helper_ids[None, :, None]).astype(jnp.float32)
    unmix = (jnp.eye(helpers, dtype=jnp.float32)[None, :, None, :] - COUPLING * coupled[..., None] * choose) / (
        1.0 - COUPLING * COUPLING
    )
    sectioned = jnp.einsum("sth,shzg->sztg", decode_block, unmix, precision=HIGHEST)
    sub_count = plane_count * group_size
    rows_in = jnp.arange(device_count * plane_count, dtype=jnp.int32)
    at_row = (sources.reshape(stripes_here, helpers)[..., None] == rows_in // plane_count).astype(jnp.float32)
    spread = jnp.einsum(
        "sag,sgr->sar", sectioned.reshape(stripes_here, sub_count, helpers), at_row, precision=HIGHEST
    )
    same_plane = jnp.arange(sub_count, dtype=jnp.int32)[:, None] // group_size == rows_in[None, :] % plane_count
    spread = jnp.where(same_plane[None], spread, 0.0)
    sub_ids = jnp.arange(sub_count, dtype=jnp.int32)
    pick = (recouple_pairs[..., None] == sub_ids).astype(jnp.float32)
    distinct = (recouple_pairs != sub_ids[None, :]).astype(jnp.float32)
    mixing = jnp.eye(sub_count, dtype=jnp.float32)[None] + COUPLING * distinct[..., None] * pick
    whole = jnp.einsum("sab,sbc->sac", mixing, spread, precision=HIGHEST)
    return whole.reshape(stripes_here * sub_count, device_count * plane_count)


def body(span_store, helper_offset, plane_index, coupling_pair, decode_matrix, recouple_pair):
    dev_count = lax.axis_size("dev")
    device_count = lax.axis_size("rack") * dev_count
    myself = lax.axis_index("rack") * dev_count + lax.axis_index("dev")
    slots, sub_total, columns = span_store.shape
    stripes_here, helpers, plane_count = coupling_pair.shape
    sub_count = recouple_pair.shape[1]
    peer_ids = jnp.arange(device_count, dtype=jnp.int32)
    slot_ids = jnp.arange(slots, dtype=jnp.int32)
    wanted = (myself - peer_ids) % device_count
    slot_of = jnp.sum(jnp.where(wanted[:, None] == helper_offset[None, :], slot_ids[None, :], 0), axis=1)
    stripe_of = slot_of // helpers
    at_stripe = (stripe_of[:, None] == jnp.arange(stripes_here, dtype=jnp.int32)).astype(jnp.int32)
    planes = jnp.sum(
        plane_index.reshape(device_count, stripes_here, plane_count) * at_stripe[..., None], axis=1
    )
    flat_rows = span_store.reshape(slots * sub_total, columns)
    row_index = (slot_of[:, None] * sub_total + planes).reshape(-1)
    outgoing = jnp.take(flat_rows, row_index, axis=0, mode="clip").reshape(device_count, plane_count, columns)
    arrived = lax.all_to_all(outgoing, ("rack", "dev"), split_axis=0, concat_axis=0, tiled=True)
    sources = (myself + helper_offset) % device_count
    whole = repair_matrix(decode_matrix, coupling_pair, recouple_pair, sources, device_count)
    rows = arrived.reshape(device_count * plane_count, columns)
    result = jnp.dot(whole, rows.astype(jnp.float32), precision=HIGHEST)
    return result.astype(jnp.bfloat16).reshape(stripes_here, sub_count, columns)


def solution(mesh):
    split = ("rack", "dev")
    placed = (
        P(split, None, None),
        P(),
        P(),
        P(split, None, None),
        P(split, None, None),
        P(split, None),
    )
    return jax.shard_map(body, mesh=mesh, in_specs=placed, out_specs=P(split, None, None), check_vma=False)
```

```python
import functools

import jax
import jax.numpy as jnp
from jax import lax
from jax.experimental import pallas as pl
from jax.experimental.pallas import tpu as pltpu
from jax.sharding import PartitionSpec as P

AXES = ("rack", "dev")
COUPLING = 0.6
HIGHEST = lax.Precision.HIGHEST
TOGETHER = 8
HBM = pl.BlockSpec(memory_space=pltpu.HBM)
VMEM = pl.BlockSpec(memory_space=pltpu.VMEM)


def near_masks(rack_count):
    return list(range(rack_count - 2, 0, -1))


def far_peer(me, index, rack_count, dev_count):
    if rack_count == 1:
        return index
    rack = me // dev_count
    first = jnp.minimum(rack, (rack_count - 1) - rack)
    rank = first if index % 2 == 0 else (rack_count - 1) - first
    return rank * dev_count + index // 2


def far_rules(rack_count, dev_count):
    size = dev_count * (2 if rack_count > 1 else 1)
    return [functools.partial(lambda i, me: far_peer(me, i, rack_count, dev_count), i) for i in range(size)]


def near_rules(mask, dev_count):
    return [functools.partial(lambda m, me: me ^ m, mask * dev_count + d) for d in range(dev_count)]


def pick_kernel(layout, in_hbm, helpers, offset_hbm, planes_hbm, store_ref, *refs):
    outs = refs[: len(layout)]
    held, staged, offset, planes, table, load_sem, store_sem, small_sem = refs[len(layout) :]
    slots, sub_total, _ = store_ref.shape
    plane_count = planes.shape[0]
    device_count = table.shape[0]
    small = [
        pltpu.make_async_copy(offset_hbm, offset, small_sem.at[0]),
        pltpu.make_async_copy(planes_hbm, planes, small_sem.at[1]),
    ]
    for copy in small:
        copy.start()
    me = lax.axis_index("rack") * lax.axis_size("dev") + lax.axis_index("dev")
    row = lax.broadcasted_iota(jnp.int32, (plane_count, sub_total), 0)
    col = lax.broadcasted_iota(jnp.int32, (plane_count, sub_total), 1)
    coarse, fine = row // 4, row % 4
    for i in range(device_count):
        table[i] = -1
    small[0].wait()
    for j in range(slots):
        table[offset[j]] = j
    order = sorted(range(len(layout)), key=lambda o: o not in in_hbm)
    blocks = [(o, k, rule) for o in order for k, rule in enumerate(layout[o])]
    wanted = []
    for b, (_, _, rule) in enumerate(blocks):
        peer = rule(me)
        gap = me - peer
        found = table[jnp.where(gap < 0, gap + device_count, gap)]
        slot = jnp.maximum(found, 0)
        copy = pltpu.make_async_copy(store_ref.at[slot], held.at[b], load_sem.at[b])
        wanted.append((found >= 0, peer * (slots // helpers) + slot // helpers, copy))

        @pl.when(found >= 0)
        def _():
            copy.start()

    small[1].wait()
    stores = []
    for first in range(0, len(blocks), TOGETHER):
        some = range(first, min(first + TOGETHER, len(blocks)))
        for b in some:
            used, _, copy = wanted[b]

            @pl.when(used)
            def _():
                copy.wait()

        for b in some:
            used, stripe, _ = wanted[b]
            o, k, _ = blocks[b]
            start, step, jump = planes[0, stripe], planes[1, stripe], planes[4, stripe]
            picked = (col == start + (jump - start) * coarse + (step - start) * fine).astype(jnp.float32)
            rows = jnp.dot(picked.astype(held.dtype), held[b], preferred_element_type=jnp.float32)
            rows = jnp.where(used, rows, 0.0).astype(held.dtype)
            into = staged if o in in_hbm else outs[o]
            into[pl.ds(k * plane_count, plane_count)] = rows
        done = [b for b in some if blocks[b][0] in in_hbm]
        if done:
            part = pl.ds(done[0] * plane_count, len(done) * plane_count)
            stores.append(pltpu.make_async_copy(staged.at[part], outs[order[0]].at[part], store_sem.at[len(stores)]))
            stores[-1].start()
    for copy in stores:
        copy.wait()


def pick_rows(layout, in_hbm, helpers, device_count, helper_offset, planes, store):
    _, sub_total, columns = store.shape
    plane_count = planes.shape[0]
    total = sum(len(rules) for rules in layout)
    direct = max([len(layout[o]) for o in in_hbm], default=1)
    return pl.pallas_call(
        functools.partial(pick_kernel, layout, in_hbm, helpers),
        out_shape=[jax.ShapeDtypeStruct((len(rules) * plane_count, columns), store.dtype) for rules in layout],
        in_specs=[HBM] * 3,
        out_specs=[HBM if o in in_hbm else VMEM for o in range(len(layout))],
        scratch_shapes=[
            pltpu.VMEM((total, sub_total, columns), store.dtype),
            pltpu.VMEM((direct * plane_count, columns), store.dtype),
            pltpu.SMEM(helper_offset.shape, jnp.int32),
            pltpu.SMEM(planes.shape, jnp.int32),
            pltpu.SMEM((device_count,), jnp.int32),
            pltpu.SemaphoreType.DMA((total,)),
            pltpu.SemaphoreType.DMA((pl.cdiv(direct, TOGETHER),)),
            pltpu.SemaphoreType.DMA((2,)),
        ],
        cost_estimate=pl.CostEstimate(
            flops=2 * total * plane_count * sub_total * columns,
            bytes_accessed=2 * total * (sub_total + plane_count) * columns,
            transcendentals=0,
        ),
        compiler_params=pltpu.CompilerParams(
            vmem_limit_bytes=2 * total * (sub_total + 3 * plane_count) * columns + (4 << 20)
        ),
        name="pick_rows",
    )(*(pltpu.with_memory_space_constraint(x, pltpu.HBM) for x in (helper_offset, planes, store)))


def rebuild_kernel(counts, matrix_ref, *refs):
    rows_refs, (out_ref, *scratch) = refs[: len(counts)], refs[len(counts) :]
    out_rows = out_ref.shape[0]
    rows = rows_refs[0]
    if len(counts) > 1:
        rows, at = scratch[0], 0
        for r, count in zip(rows_refs, counts):
            rows[pl.ds(at, count)] = r[pl.ds(0, count)]
            at += count
    three = jnp.dot(matrix_ref[...], rows[...], preferred_element_type=jnp.float32)
    total = three[2 * out_rows :] + three[out_rows : 2 * out_rows] + three[:out_rows]
    out_ref[...] = total.astype(out_ref.dtype)


def rebuild(matrix, pieces, counts):
    out_rows = matrix.shape[0] // 3
    columns = pieces[0].shape[1]
    total = sum(counts)
    return pl.pallas_call(
        functools.partial(rebuild_kernel, counts),
        out_shape=jax.ShapeDtypeStruct((out_rows, columns), jnp.bfloat16),
        in_specs=[VMEM] * (1 + len(pieces)),
        out_specs=VMEM,
        scratch_shapes=[pltpu.VMEM((total, columns), jnp.bfloat16)] if len(pieces) > 1 else [],
        cost_estimate=pl.CostEstimate(
            flops=6 * out_rows * total * columns, bytes_accessed=2 * columns * (total + out_rows), transcendentals=0
        ),
        compiler_params=pltpu.CompilerParams(vmem_limit_bytes=(4 * total + 16 * out_rows) * columns + (4 << 20)),
        name="rebuild",
    )(matrix, *pieces)


def three_terms(x):
    terms = []
    for _ in range(3):
        terms.append(lax.reduce_precision(x, 8, 7))
        x = x - terms[-1]
    return jnp.concatenate(terms, 0).astype(jnp.bfloat16)


def repair_matrix(decode_block, pair_block, recouple_pairs, sources, peers):
    stripes_here, helpers, plane_count = pair_block.shape
    group_size = decode_block.shape[1]
    helper_ids = jnp.arange(helpers, dtype=jnp.int32)
    choose = (pair_block[..., None] == helper_ids).astype(jnp.float32)
    coupled = (pair_block != helper_ids[None, :, None]).astype(jnp.float32)
    unmix = (jnp.eye(helpers, dtype=jnp.float32)[None, :, None, :] - COUPLING * coupled[..., None] * choose) / (
        1.0 - COUPLING * COUPLING
    )
    sectioned = jnp.einsum("sth,shzg->sztg", decode_block, unmix, precision=HIGHEST)
    sub_count = plane_count * group_size
    rows_in = jnp.arange(peers.shape[0] * plane_count, dtype=jnp.int32)
    peer_of_row = jnp.repeat(peers, plane_count)
    at_row = (sources.reshape(stripes_here, helpers)[..., None] == peer_of_row).astype(jnp.float32)
    spread = jnp.einsum(
        "sag,sgr->sar", sectioned.reshape(stripes_here, sub_count, helpers), at_row, precision=HIGHEST
    )
    same_plane = jnp.arange(sub_count, dtype=jnp.int32)[:, None] // group_size == rows_in[None, :] % plane_count
    spread = jnp.where(same_plane[None], spread, 0.0)
    sub_ids = jnp.arange(sub_count, dtype=jnp.int32)
    pick = (recouple_pairs[..., None] == sub_ids).astype(jnp.float32)
    distinct = (recouple_pairs != sub_ids[None, :]).astype(jnp.float32)
    mixing = jnp.eye(sub_count, dtype=jnp.float32)[None] + COUPLING * distinct[..., None] * pick
    whole = jnp.einsum("sab,sbc->sac", mixing, spread, precision=HIGHEST)
    return whole.reshape(stripes_here * sub_count, peers.shape[0] * plane_count)


def swap(x, mask, device_count):
    return lax.ppermute(x, AXES, [(q, q ^ mask) for q in range(device_count)])


def body(span_store, helper_offset, plane_index, coupling_pair, decode_matrix, recouple_pair):
    rack_count, dev_count = lax.axis_size("rack"), lax.axis_size("dev")
    device_count = rack_count * dev_count
    me = lax.axis_index("rack") * dev_count + lax.axis_index("dev")
    columns = span_store.shape[-1]
    stripes_here, helpers, plane_count = coupling_pair.shape
    sub_count = recouple_pair.shape[1]
    near = near_masks(rack_count)
    pick = functools.partial(
        pick_rows, helpers=helpers, device_count=device_count, helper_offset=helper_offset, planes=plane_index.T, store=span_store
    )
    early = near[:2]
    outgoing = []
    if early:
        outgoing += pick([near_rules(m, dev_count) for m in early], ())
    layout = [near_rules(m, dev_count) for m in near[len(early):]] + [far_rules(rack_count, dev_count)]
    outgoing += pick(layout, (len(layout) - 1,))
    across = [swap(x, m * dev_count, device_count) for m, x in zip(near, outgoing)]
    groups = None
    if rack_count > 1:
        groups = [
            [rack * dev_count + d for d in range(dev_count) for rack in (r, rack_count - 1 - r)]
            for r in range(rack_count // 2)
        ]
    blocks = outgoing[-1].reshape(-1, plane_count, columns)
    far = lax.all_to_all(blocks, AXES, 0, 0, axis_index_groups=groups, tiled=True).reshape(-1, columns)
    peers = [far_peer(me, i, rack_count, dev_count) for i in range(far.shape[0] // plane_count)]
    arrived, counts = [far], [far.shape[0]]
    if near:
        chips = range(dev_count // 2)
        blocks = [x.reshape(-1, 2, plane_count, columns) for x in across]
        crossed = swap(jnp.concatenate([x[chip, 1] for chip in chips for x in blocks], 0), 1, device_count)
        both = len(near) * plane_count
        arrived += across + [crossed]
        counts += [plane_count] * len(near) + [both]
        peers += [me ^ (m * dev_count) for m in near] + [me ^ (m * dev_count) ^ 1 for m in near]
        for chip in chips[1:]:
            part = [x[chip, 0] for x in blocks] + [crossed[both * chip : both * (chip + 1)]]
            arrived.append(swap(jnp.concatenate(part, 0), 2 * chip, device_count))
            counts.append(2 * both)
            peers += [me ^ (m * dev_count + 2 * chip + core) for core in (0, 1) for m in near]
    sources = (me + helper_offset) % device_count
    peers = jnp.stack([jnp.asarray(p, jnp.int32) for p in peers])
    whole = three_terms(repair_matrix(decode_matrix, coupling_pair, recouple_pair, sources, peers))
    return rebuild(whole, arrived, counts).reshape(stripes_here, sub_count, columns)


def solution(mesh):
    split = ("rack", "dev")
    placed = (
        P(split, None, None),
        P(),
        P(),
        P(split, None, None),
        P(split, None, None),
        P(split, None),
    )
    return jax.shard_map(body, mesh=mesh, in_specs=placed, out_specs=P(split, None, None), check_vma=False)
```

```python
import functools

import jax
import jax.numpy as jnp
from jax import lax
from jax.experimental import pallas as pl
from jax.experimental.pallas import tpu as pltpu
from jax.sharding import PartitionSpec as P

AXES = ("rack", "dev")
COUPLING = 0.6
HIGHEST = lax.Precision.HIGHEST
TOGETHER = 8
AHEAD = 2
TERMS = 3
PARTS = 2
HBM = pl.BlockSpec(memory_space=pltpu.HBM)
VMEM = pl.BlockSpec(memory_space=pltpu.VMEM)


def near_masks(rack_count):
    return list(range(rack_count - 2, 0, -1))


def far_peer(me, index, rack_count, dev_count):
    if rack_count == 1:
        return index
    rack = me // dev_count
    first = jnp.minimum(rack, (rack_count - 1) - rack)
    rank = first if index % 2 == 0 else (rack_count - 1) - first
    return rank * dev_count + index // 2


def ahead_chips(rack_count, dev_count):
    chips = dev_count // 2
    return list(range(chips - min(AHEAD, chips - 1), chips)) if near_masks(rack_count) else []


def outgoing_rules(near, ahead, rack_count, dev_count):
    def to(mask):
        return lambda me: me ^ mask

    counts = [dev_count - 2 * len(ahead)] + [dev_count] * (len(near) - 1) if near else []
    rules = [[to(m * dev_count + d) for d in range(count)] for m, count in zip(near, counts)]
    rules += [[to(near[0] * dev_count + 2 * chip + core) for core in (0, 1)] for chip in ahead]
    far_count = dev_count * (2 if rack_count > 1 else 1)
    rules.append([functools.partial(far_peer, index=i, rack_count=rack_count, dev_count=dev_count) for i in range(far_count)])
    return rules


def pick_kernel(rules, helpers, offset_hbm, planes_hbm, store_ref, *refs):
    outs, (held, picked, offset, planes, table, load_sem, small_sem) = refs[:-7], refs[-7:]
    slots, sub_total, _ = store_ref.shape
    plane_count = planes.shape[0]
    device_count = table.shape[0]
    small = [
        pltpu.make_async_copy(offset_hbm, offset, small_sem.at[0]),
        pltpu.make_async_copy(planes_hbm, planes, small_sem.at[1]),
    ]
    loads = [pltpu.make_async_copy(store_ref.at[j], held.at[j], load_sem.at[j]) for j in range(slots)]
    for copy in small + loads:
        copy.start()
    me = lax.axis_index("rack") * lax.axis_size("dev") + lax.axis_index("dev")
    row = lax.broadcasted_iota(jnp.int32, (plane_count, sub_total), 0)
    col = lax.broadcasted_iota(jnp.int32, (plane_count, sub_total), 1)
    coarse, fine = row // 4, row % 4
    for i in range(device_count):
        table[i] = -1
    for copy in small:
        copy.wait()
    wanted = []
    for j in range(slots):
        gap = me - offset[j]
        peer = jnp.where(gap < 0, gap + device_count, gap)
        table[peer] = j
        stripe = peer * (slots // helpers) + j // helpers
        start = planes[0, stripe]
        wanted.append((start, planes[1, stripe] - start, planes[4, stripe] - start))
    for first in range(0, slots, TOGETHER):
        some = range(first, min(first + TOGETHER, slots))
        for j in some:
            loads[j].wait()
        for j in some:
            start, step, jump = wanted[j]
            mask = (col == start + jump * coarse + step * fine).astype(jnp.float32)
            rows = jnp.dot(mask.astype(held.dtype), held[j], preferred_element_type=jnp.float32)
            picked[j] = rows.astype(held.dtype)
    for out, receivers in zip(outs, rules):
        for k, receiver in enumerate(receivers):
            slot = table[receiver(me)]
            rows = jnp.where(slot >= 0, picked[jnp.maximum(slot, 0)], jnp.zeros((), held.dtype))
            out[pl.ds(k * plane_count, plane_count)] = rows


def pick_rows(rules, helpers, device_count, helper_offset, planes, store):
    slots, sub_total, columns = store.shape
    plane_count = planes.shape[0]
    counts = [len(r) * plane_count for r in rules]
    return pl.pallas_call(
        functools.partial(pick_kernel, rules, helpers),
        out_shape=[jax.ShapeDtypeStruct((count, columns), store.dtype) for count in counts],
        in_specs=[HBM] * 3,
        out_specs=[VMEM] * len(counts),
        scratch_shapes=[
            pltpu.VMEM((slots, sub_total, columns), store.dtype),
            pltpu.VMEM((slots, plane_count, columns), store.dtype),
            pltpu.SMEM(helper_offset.shape, jnp.int32),
            pltpu.SMEM(planes.shape, jnp.int32),
            pltpu.SMEM((device_count,), jnp.int32),
            pltpu.SemaphoreType.DMA((slots,)),
            pltpu.SemaphoreType.DMA((2,)),
        ],
        cost_estimate=pl.CostEstimate(
            flops=2 * slots * plane_count * sub_total * columns,
            bytes_accessed=2 * (slots * sub_total + sum(counts)) * columns,
            transcendentals=0,
        ),
        compiler_params=pltpu.CompilerParams(
            vmem_limit_bytes=2 * (slots * (sub_total + plane_count) + 2 * sum(counts)) * columns + (4 << 20)
        ),
        name="pick_rows",
    )(*(pltpu.with_memory_space_constraint(x, pltpu.HBM) for x in (helper_offset, planes, store)))


def put_kernel(rows_ref, out_ref, sem):
    copy = pltpu.make_async_copy(rows_ref, out_ref, sem)
    copy.start()
    copy.wait()


def put_in_hbm(rows):
    return pl.pallas_call(
        put_kernel,
        out_shape=jax.ShapeDtypeStruct(rows.shape, rows.dtype),
        in_specs=[VMEM],
        out_specs=HBM,
        scratch_shapes=[pltpu.SemaphoreType.DMA],
        cost_estimate=pl.CostEstimate(flops=0, bytes_accessed=4 * rows.size, transcendentals=0),
        compiler_params=pltpu.CompilerParams(vmem_limit_bytes=2 * rows.size + (4 << 20)),
        name="put_in_hbm",
    )(rows)


def rebuild_kernel(counts, matrix_ref, *refs):
    rows_refs, (out_ref, made, store_sem, *scratch) = refs[: len(counts)], refs[len(counts) :]
    out_rows = out_ref.shape[0]
    rows = rows_refs[0]
    if len(counts) > 1:
        rows, at = scratch[0], 0
        for r, count in zip(rows_refs, counts):
            rows[pl.ds(at, count)] = r[pl.ds(0, count)]
            at += count
    wide = out_ref.shape[1] // PARTS
    stores = []
    for c in range(PARTS):
        part = pl.ds(c * wide, wide)
        terms = jnp.dot(matrix_ref[...], rows[:, part], preferred_element_type=jnp.float32)
        total = terms[:out_rows]
        for t in range(1, TERMS):
            total += terms[t * out_rows : (t + 1) * out_rows]
        made[:, part] = total.astype(made.dtype)
        stores.append(pltpu.make_async_copy(made.at[:, part], out_ref.at[:, part], store_sem.at[c]))
        stores[-1].start()
    for copy in stores:
        copy.wait()


def rebuild(matrix, pieces, counts):
    out_rows = matrix.shape[0] // TERMS
    columns = pieces[0].shape[1]
    total = sum(counts)
    return pl.pallas_call(
        functools.partial(rebuild_kernel, counts),
        out_shape=jax.ShapeDtypeStruct((out_rows, columns), jnp.bfloat16),
        in_specs=[VMEM] * (1 + len(pieces)),
        out_specs=HBM,
        scratch_shapes=[pltpu.VMEM((out_rows, columns), jnp.bfloat16), pltpu.SemaphoreType.DMA((PARTS,))]
        + ([pltpu.VMEM((total, columns), jnp.bfloat16)] if len(pieces) > 1 else []),
        cost_estimate=pl.CostEstimate(
            flops=2 * TERMS * out_rows * total * columns, bytes_accessed=2 * columns * (total + out_rows), transcendentals=0
        ),
        compiler_params=pltpu.CompilerParams(vmem_limit_bytes=(4 * total + 16 * out_rows) * columns + (4 << 20)),
        name="rebuild",
    )(matrix, *pieces)


def in_terms(x):
    terms = []
    for _ in range(TERMS):
        terms.append(lax.reduce_precision(x, 8, 7))
        x = x - terms[-1]
    return jnp.concatenate(terms, 0).astype(jnp.bfloat16)


def repair_matrix(decode_block, pair_block, recouple_pairs, sources, peers):
    stripes_here, helpers, plane_count = pair_block.shape
    group_size = decode_block.shape[1]
    helper_ids = jnp.arange(helpers, dtype=jnp.int32)
    choose = (pair_block[..., None] == helper_ids).astype(jnp.float32)
    coupled = (pair_block != helper_ids[None, :, None]).astype(jnp.float32)
    unmix = (jnp.eye(helpers, dtype=jnp.float32)[None, :, None, :] - COUPLING * coupled[..., None] * choose) / (
        1.0 - COUPLING * COUPLING
    )
    sectioned = jnp.einsum("sth,shzg->sztg", decode_block, unmix, precision=HIGHEST)
    sub_count = plane_count * group_size
    rows_in = jnp.arange(peers.shape[0] * plane_count, dtype=jnp.int32)
    peer_of_row = jnp.repeat(peers, plane_count)
    at_row = (sources.reshape(stripes_here, helpers)[..., None] == peer_of_row).astype(jnp.float32)
    spread = jnp.einsum(
        "sag,sgr->sar", sectioned.reshape(stripes_here, sub_count, helpers), at_row, precision=HIGHEST
    )
    same_plane = jnp.arange(sub_count, dtype=jnp.int32)[:, None] // group_size == rows_in[None, :] % plane_count
    spread = jnp.where(same_plane[None], spread, 0.0)
    sub_ids = jnp.arange(sub_count, dtype=jnp.int32)
    pick = (recouple_pairs[..., None] == sub_ids).astype(jnp.float32)
    distinct = (recouple_pairs != sub_ids[None, :]).astype(jnp.float32)
    mixing = jnp.eye(sub_count, dtype=jnp.float32)[None] + COUPLING * distinct[..., None] * pick
    whole = jnp.einsum("sab,sbc->sac", mixing, spread, precision=HIGHEST)
    return whole.reshape(stripes_here * sub_count, peers.shape[0] * plane_count)


def swap(x, mask, device_count):
    return lax.ppermute(x, AXES, [(q, q ^ mask) for q in range(device_count)])


def body(span_store, helper_offset, plane_index, coupling_pair, decode_matrix, recouple_pair):
    rack_count, dev_count = lax.axis_size("rack"), lax.axis_size("dev")
    device_count = rack_count * dev_count
    me = lax.axis_index("rack") * dev_count + lax.axis_index("dev")
    columns = span_store.shape[-1]
    stripes_here, helpers, plane_count = coupling_pair.shape
    sub_count = recouple_pair.shape[1]
    near = near_masks(rack_count)
    ahead = ahead_chips(rack_count, dev_count)
    rules = outgoing_rules(near, ahead, rack_count, dev_count)
    outgoing = pick_rows(rules, helpers, device_count, helper_offset, plane_index.T, span_store)
    across = [swap(x, m * dev_count, device_count) for m, x in zip(near, outgoing)]
    groups = None
    if rack_count > 1:
        groups = [
            [rack * dev_count + d for d in range(dev_count) for rack in (r, rack_count - 1 - r)]
            for r in range(rack_count // 2)
        ]
    blocks = put_in_hbm(outgoing[-1]).reshape(-1, plane_count, columns)
    far = lax.all_to_all(blocks, AXES, 0, 0, axis_index_groups=groups, tiled=True).reshape(-1, columns)
    peers = [far_peer(me, i, rack_count, dev_count) for i in range(far.shape[0] // plane_count)]
    arrived, counts = [far], [far.shape[0]]
    if near:
        chips = range(dev_count // 2)
        straight = [
            swap(x, near[0] * dev_count + 2 * chip, device_count)
            for chip, x in zip(ahead, outgoing[len(near) :])
        ]
        home = [(x, m * dev_count, 0) for m, x in zip(near, across)]
        home += [(x, near[0] * dev_count + 2 * chip, 0) for chip, x in zip(ahead, straight)]
        onward = [
            [(x, m * dev_count + 2 * chip, chip) for m, x in zip(near, across) if m != near[0] or chip not in ahead]
            for chip in chips[1:]
        ]

        def block(x, index):
            return x[index * plane_count : (index + 1) * plane_count]

        crossing = [block(x, 2 * chip + 1) for x, _, chip in home + sum(onward, [])]
        crossed = swap(jnp.concatenate(crossing, 0), 1, device_count)
        arrived += [x for x, _, _ in home] + [crossed]
        counts += [plane_count] * len(home) + [len(home) * plane_count]
        peers += [me ^ mask for _, mask, _ in home] + [me ^ mask ^ 1 for _, mask, _ in home]
        at = len(home) * plane_count
        for chip, some in zip(chips[1:], onward):
            size = len(some) * plane_count
            part = [block(x, 2 * chip) for x, _, _ in some] + [crossed[at : at + size]]
            arrived.append(swap(jnp.concatenate(part, 0), 2 * chip, device_count))
            counts.append(2 * size)
            peers += [me ^ mask ^ core for core in (0, 1) for _, mask, _ in some]
            at += size
    sources = (me + helper_offset) % device_count
    peers = jnp.stack([jnp.asarray(p, jnp.int32) for p in peers])
    whole = in_terms(repair_matrix(decode_matrix, coupling_pair, recouple_pair, sources, peers))
    return rebuild(whole, arrived, counts).reshape(stripes_here, sub_count, columns)


def solution(mesh):
    split = ("rack", "dev")
    placed = (
        P(split, None, None),
        P(),
        P(),
        P(split, None, None),
        P(split, None, None),
        P(split, None),
    )
    return jax.shard_map(body, mesh=mesh, in_specs=placed, out_specs=P(split, None, None), check_vma=False)
```

```python
import functools

import jax
import jax.numpy as jnp
from jax import lax
from jax.experimental import pallas as pl
from jax.experimental.pallas import tpu as pltpu
from jax.sharding import PartitionSpec as P

AXES = ("rack", "dev")
COUPLING = 0.6
HIGHEST = lax.Precision.HIGHEST
TOGETHER = 8
AHEAD = 2
TERMS = 3
PARTS = 2
HBM = pl.BlockSpec(memory_space=pltpu.HBM)
VMEM = pl.BlockSpec(memory_space=pltpu.VMEM)


def near_masks(rack_count):
    return list(range(rack_count - 2, 0, -1))


def far_peer(me, index, rack_count, dev_count):
    if rack_count == 1:
        return index
    rack = me // dev_count
    first = jnp.minimum(rack, (rack_count - 1) - rack)
    rank = first if index % 2 == 0 else (rack_count - 1) - first
    return rank * dev_count + index // 2


def ahead_chips(rack_count, dev_count):
    chips = dev_count // 2
    return list(range(chips - min(AHEAD, chips - 1), chips)) if near_masks(rack_count) else []


def outgoing_rules(near, ahead, rack_count, dev_count):
    def to(mask):
        return lambda me: me ^ mask

    counts = [dev_count - 2 * len(ahead)] + [dev_count] * (len(near) - 1) if near else []
    rules = [[to(m * dev_count + d) for d in range(count)] for m, count in zip(near, counts)]
    rules += [[to(near[0] * dev_count + 2 * chip + core) for core in (0, 1)] for chip in ahead]
    far_count = dev_count * (2 if rack_count > 1 else 1)
    rules.append([functools.partial(far_peer, index=i, rack_count=rack_count, dev_count=dev_count) for i in range(far_count)])
    return rules


def pick_kernel(rules, helpers, offset_hbm, planes_hbm, store_ref, *refs):
    outs, (held, picked, offset, planes, table, load_sem, small_sem) = refs[:-7], refs[-7:]
    slots, sub_total, _ = store_ref.shape
    plane_count = planes.shape[0]
    device_count = table.shape[0]
    small = [
        pltpu.make_async_copy(offset_hbm, offset, small_sem.at[0]),
        pltpu.make_async_copy(planes_hbm, planes, small_sem.at[1]),
    ]
    loads = [pltpu.make_async_copy(store_ref.at[j], held.at[j], load_sem.at[j]) for j in range(slots)]
    for copy in small + loads:
        copy.start()
    me = lax.axis_index("rack") * lax.axis_size("dev") + lax.axis_index("dev")
    row = lax.broadcasted_iota(jnp.int32, (plane_count, sub_total), 0)
    col = lax.broadcasted_iota(jnp.int32, (plane_count, sub_total), 1)
    coarse, fine = row // 4, row % 4
    for i in range(device_count):
        table[i] = -1
    for copy in small:
        copy.wait()
    wanted = []
    for j in range(slots):
        gap = me - offset[j]
        peer = jnp.where(gap < 0, gap + device_count, gap)
        table[peer] = j
        stripe = peer * (slots // helpers) + j // helpers
        start = planes[0, stripe]
        wanted.append((start, planes[1, stripe] - start, planes[4, stripe] - start))
    for first in range(0, slots, TOGETHER):
        some = range(first, min(first + TOGETHER, slots))
        for j in some:
            loads[j].wait()
        for j in some:
            start, step, jump = wanted[j]
            mask = (col == start + jump * coarse + step * fine).astype(jnp.float32)
            rows = jnp.dot(mask.astype(held.dtype), held[j], preferred_element_type=jnp.float32)
            picked[j] = rows.astype(held.dtype)
    for out, receivers in zip(outs, rules):
        for k, receiver in enumerate(receivers):
            slot = table[receiver(me)]
            rows = jnp.where(slot >= 0, picked[jnp.maximum(slot, 0)], jnp.zeros((), held.dtype))
            out[pl.ds(k * plane_count, plane_count)] = rows


def pick_rows(rules, helpers, device_count, helper_offset, planes, store):
    slots, sub_total, columns = store.shape
    plane_count = planes.shape[0]
    counts = [len(r) * plane_count for r in rules]
    return pl.pallas_call(
        functools.partial(pick_kernel, rules, helpers),
        out_shape=[jax.ShapeDtypeStruct((count, columns), store.dtype) for count in counts],
        in_specs=[HBM] * 3,
        out_specs=[VMEM] * len(counts),
        scratch_shapes=[
            pltpu.VMEM((slots, sub_total, columns), store.dtype),
            pltpu.VMEM((slots, plane_count, columns), store.dtype),
            pltpu.SMEM(helper_offset.shape, jnp.int32),
            pltpu.SMEM(planes.shape, jnp.int32),
            pltpu.SMEM((device_count,), jnp.int32),
            pltpu.SemaphoreType.DMA((slots,)),
            pltpu.SemaphoreType.DMA((2,)),
        ],
        cost_estimate=pl.CostEstimate(
            flops=2 * slots * plane_count * sub_total * columns,
            bytes_accessed=2 * (slots * sub_total + sum(counts)) * columns,
            transcendentals=0,
        ),
        compiler_params=pltpu.CompilerParams(
            vmem_limit_bytes=2 * (slots * (sub_total + plane_count) + 2 * sum(counts)) * columns + (4 << 20)
        ),
        name="pick_rows",
    )(*(pltpu.with_memory_space_constraint(x, pltpu.HBM) for x in (helper_offset, planes, store)))


def put_kernel(rows_ref, out_ref, sem):
    copy = pltpu.make_async_copy(rows_ref, out_ref, sem)
    copy.start()
    copy.wait()


def put_in_hbm(rows):
    return pl.pallas_call(
        put_kernel,
        out_shape=jax.ShapeDtypeStruct(rows.shape, rows.dtype),
        in_specs=[VMEM],
        out_specs=HBM,
        scratch_shapes=[pltpu.SemaphoreType.DMA],
        cost_estimate=pl.CostEstimate(flops=0, bytes_accessed=4 * rows.size, transcendentals=0),
        compiler_params=pltpu.CompilerParams(vmem_limit_bytes=2 * rows.size + (4 << 20)),
        name="put_in_hbm",
    )(rows)


def gather_rows(scratch, rows_refs, counts):
    at = 0
    for r, count in zip(rows_refs, counts):
        scratch[pl.ds(at, count)] = r[pl.ds(0, count)]
        at += count


def add_terms(terms, out_rows):
    total = terms[:out_rows]
    for t in range(1, TERMS):
        total += terms[t * out_rows : (t + 1) * out_rows]
    return total


def begin_kernel(counts, matrix_ref, *refs):
    rows_refs, (out_ref, rows) = refs[: len(counts)], refs[len(counts) :]
    gather_rows(rows, rows_refs, counts)
    terms = jnp.dot(matrix_ref[:, : rows.shape[0]], rows[...], preferred_element_type=jnp.float32)
    out_ref[...] = add_terms(terms, out_ref.shape[0])


def finish_kernel(counts, skip, matrix_ref, begun_ref, *refs):
    rows_refs, (out_ref, made, rows, store_sem) = refs[: len(counts)], refs[len(counts) :]
    out_rows, columns = out_ref.shape
    gather_rows(rows, rows_refs, counts)
    wide = columns // PARTS
    stores = []
    for c in range(PARTS):
        part = pl.ds(c * wide, wide)
        total = begun_ref[:, part]
        if counts:
            terms = jnp.dot(matrix_ref[:, skip:], rows[:, part], preferred_element_type=jnp.float32)
            total += add_terms(terms, out_rows)
        made[:, part] = total.astype(made.dtype)
        stores.append(pltpu.make_async_copy(made.at[:, part], out_ref.at[:, part], store_sem.at[c]))
        stores[-1].start()
    for copy in stores:
        copy.wait()


def rebuild(matrix, pieces, counts, split):
    out_rows = matrix.shape[0] // TERMS
    columns = pieces[0].shape[1]
    early, late = sum(counts[:split]), sum(counts[split:])

    def settings(rows):
        return dict(
            cost_estimate=pl.CostEstimate(
                flops=2 * TERMS * out_rows * rows * columns,
                bytes_accessed=2 * columns * (rows + out_rows),
                transcendentals=0,
            ),
            compiler_params=pltpu.CompilerParams(
                vmem_limit_bytes=(4 * rows + 16 * out_rows) * columns + 4 * matrix.size + (4 << 20)
            ),
        )

    begun = pl.pallas_call(
        functools.partial(begin_kernel, counts[:split]),
        out_shape=jax.ShapeDtypeStruct((out_rows, columns), jnp.float32),
        in_specs=[VMEM] * (1 + split),
        out_specs=VMEM,
        scratch_shapes=[pltpu.VMEM((early, columns), jnp.bfloat16)],
        name="begin",
        **settings(early),
    )(matrix, *pieces[:split])
    return pl.pallas_call(
        functools.partial(finish_kernel, counts[split:], early),
        out_shape=jax.ShapeDtypeStruct((out_rows, columns), jnp.bfloat16),
        in_specs=[VMEM] * (2 + len(pieces) - split),
        out_specs=HBM,
        scratch_shapes=[
            pltpu.VMEM((out_rows, columns), jnp.bfloat16),
            pltpu.VMEM((max(late, 16), columns), jnp.bfloat16),
            pltpu.SemaphoreType.DMA((PARTS,)),
        ],
        name="finish",
        **settings(late),
    )(matrix, begun, *pieces[split:])


def in_terms(x):
    terms = []
    for _ in range(TERMS):
        terms.append(lax.reduce_precision(x, 8, 7))
        x = x - terms[-1]
    return jnp.concatenate(terms, 0).astype(jnp.bfloat16)


def repair_matrix(decode_block, pair_block, recouple_pairs, sources, peers):
    stripes_here, helpers, plane_count = pair_block.shape
    group_size = decode_block.shape[1]
    helper_ids = jnp.arange(helpers, dtype=jnp.int32)
    choose = (pair_block[..., None] == helper_ids).astype(jnp.float32)
    coupled = (pair_block != helper_ids[None, :, None]).astype(jnp.float32)
    unmix = (jnp.eye(helpers, dtype=jnp.float32)[None, :, None, :] - COUPLING * coupled[..., None] * choose) / (
        1.0 - COUPLING * COUPLING
    )
    sectioned = jnp.einsum("sth,shzg->sztg", decode_block, unmix, precision=HIGHEST)
    sub_count = plane_count * group_size
    rows_in = jnp.arange(peers.shape[0] * plane_count, dtype=jnp.int32)
    peer_of_row = jnp.repeat(peers, plane_count)
    at_row = (sources.reshape(stripes_here, helpers)[..., None] == peer_of_row).astype(jnp.float32)
    spread = jnp.einsum(
        "sag,sgr->sar", sectioned.reshape(stripes_here, sub_count, helpers), at_row, precision=HIGHEST
    )
    same_plane = jnp.arange(sub_count, dtype=jnp.int32)[:, None] // group_size == rows_in[None, :] % plane_count
    spread = jnp.where(same_plane[None], spread, 0.0)
    sub_ids = jnp.arange(sub_count, dtype=jnp.int32)
    pick = (recouple_pairs[..., None] == sub_ids).astype(jnp.float32)
    distinct = (recouple_pairs != sub_ids[None, :]).astype(jnp.float32)
    mixing = jnp.eye(sub_count, dtype=jnp.float32)[None] + COUPLING * distinct[..., None] * pick
    whole = jnp.einsum("sab,sbc->sac", mixing, spread, precision=HIGHEST)
    return whole.reshape(stripes_here * sub_count, peers.shape[0] * plane_count)


def swap(x, mask, device_count):
    return lax.ppermute(x, AXES, [(q, q ^ mask) for q in range(device_count)])


def body(span_store, helper_offset, plane_index, coupling_pair, decode_matrix, recouple_pair):
    rack_count, dev_count = lax.axis_size("rack"), lax.axis_size("dev")
    device_count = rack_count * dev_count
    me = lax.axis_index("rack") * dev_count + lax.axis_index("dev")
    columns = span_store.shape[-1]
    stripes_here, helpers, plane_count = coupling_pair.shape
    sub_count = recouple_pair.shape[1]
    near = near_masks(rack_count)
    ahead = ahead_chips(rack_count, dev_count)
    rules = outgoing_rules(near, ahead, rack_count, dev_count)
    outgoing = pick_rows(rules, helpers, device_count, helper_offset, plane_index.T, span_store)
    across = [swap(x, m * dev_count, device_count) for m, x in zip(near, outgoing)]
    groups = None
    if rack_count > 1:
        groups = [
            [rack * dev_count + d for d in range(dev_count) for rack in (r, rack_count - 1 - r)]
            for r in range(rack_count // 2)
        ]
    blocks = put_in_hbm(outgoing[-1]).reshape(-1, plane_count, columns)
    far = lax.all_to_all(blocks, AXES, 0, 0, axis_index_groups=groups, tiled=True).reshape(-1, columns)
    peers = [far_peer(me, i, rack_count, dev_count) for i in range(far.shape[0] // plane_count)]
    arrived, counts = [far], [far.shape[0]]
    if near:
        chips = range(dev_count // 2)
        straight = [
            swap(x, near[0] * dev_count + 2 * chip, device_count)
            for chip, x in zip(ahead, outgoing[len(near) :])
        ]
        home = [(x, m * dev_count, 0) for m, x in zip(near, across)]
        home += [(x, near[0] * dev_count + 2 * chip, 0) for chip, x in zip(ahead, straight)]
        onward = [
            [(x, m * dev_count + 2 * chip, chip) for m, x in zip(near, across) if m != near[0] or chip not in ahead]
            for chip in chips[1:]
        ]

        def block(x, index):
            return x[index * plane_count : (index + 1) * plane_count]

        crossing = [block(x, 2 * chip + 1) for x, _, chip in home + sum(onward, [])]
        crossed = swap(jnp.concatenate(crossing, 0), 1, device_count)
        arrived += [x for x, _, _ in home] + [crossed]
        counts += [plane_count] * len(home) + [len(home) * plane_count]
        peers += [me ^ mask for _, mask, _ in home] + [me ^ mask ^ 1 for _, mask, _ in home]
        at = len(home) * plane_count
        for chip, some in zip(chips[1:], onward):
            size = len(some) * plane_count
            part = [block(x, 2 * chip) for x, _, _ in some] + [crossed[at : at + size]]
            arrived.append(swap(jnp.concatenate(part, 0), 2 * chip, device_count))
            counts.append(2 * size)
            peers += [me ^ mask ^ core for core in (0, 1) for _, mask, _ in some]
            at += size
    split = len(arrived) - (dev_count // 2 - 1 if near else 0)
    sources = (me + helper_offset) % device_count
    peers = jnp.stack([jnp.asarray(p, jnp.int32) for p in peers])
    whole = in_terms(repair_matrix(decode_matrix, coupling_pair, recouple_pair, sources, peers))
    return rebuild(whole, arrived, counts, split).reshape(stripes_here, sub_count, columns)


def solution(mesh):
    split = ("rack", "dev")
    placed = (
        P(split, None, None),
        P(),
        P(),
        P(split, None, None),
        P(split, None, None),
        P(split, None),
    )
    return jax.shard_map(body, mesh=mesh, in_specs=placed, out_specs=P(split, None, None), check_vma=False)
```

```python
import functools

import jax
import jax.numpy as jnp
from jax import lax
from jax.experimental import pallas as pl
from jax.experimental.pallas import tpu as pltpu
from jax.sharding import PartitionSpec as P

AXES = ("rack", "dev")
COUPLING = 0.6
HIGHEST = lax.Precision.HIGHEST
TOGETHER = 8
AHEAD = 2
TERMS = 3
PARTS = 1
HBM = pl.BlockSpec(memory_space=pltpu.HBM)
VMEM = pl.BlockSpec(memory_space=pltpu.VMEM)


def near_masks(rack_count):
    return list(range(rack_count - 2, 0, -1))


def far_peer(me, index, rack_count, dev_count):
    if rack_count == 1:
        return index
    rack = me // dev_count
    first = jnp.minimum(rack, (rack_count - 1) - rack)
    rank = first if index % 2 == 0 else (rack_count - 1) - first
    return rank * dev_count + index // 2


def ahead_chips(rack_count, dev_count):
    chips = dev_count // 2
    return list(range(chips - min(AHEAD, chips - 1), chips)) if near_masks(rack_count) else []


def outgoing_rules(near, ahead, rack_count, dev_count):
    def to(mask):
        return lambda me: me ^ mask

    counts = [dev_count - 2 * len(ahead)] + [dev_count] * (len(near) - 1) if near else []
    rules = [[to(m * dev_count + d) for d in range(count)] for m, count in zip(near, counts)]
    rules += [[to(near[0] * dev_count + 2 * chip + core) for core in (0, 1)] for chip in ahead]
    far_count = dev_count * (2 if rack_count > 1 else 1)
    rules.append([functools.partial(far_peer, index=i, rack_count=rack_count, dev_count=dev_count) for i in range(far_count)])
    return rules


def pick_kernel(rules, helpers, offset_hbm, planes_hbm, store_ref, *refs):
    outs, (held, picked, offset, planes, table, load_sem, small_sem) = refs[:-7], refs[-7:]
    slots, sub_total, _ = store_ref.shape
    plane_count = planes.shape[0]
    device_count = table.shape[0]
    small = [
        pltpu.make_async_copy(offset_hbm, offset, small_sem.at[0]),
        pltpu.make_async_copy(planes_hbm, planes, small_sem.at[1]),
    ]
    loads = [pltpu.make_async_copy(store_ref.at[j], held.at[j], load_sem.at[j]) for j in range(slots)]
    for copy in small + loads:
        copy.start()
    me = lax.axis_index("rack") * lax.axis_size("dev") + lax.axis_index("dev")
    row = lax.broadcasted_iota(jnp.int32, (plane_count, sub_total), 0)
    col = lax.broadcasted_iota(jnp.int32, (plane_count, sub_total), 1)
    coarse, fine = row // 4, row % 4
    for i in range(device_count):
        table[i] = -1
    for copy in small:
        copy.wait()
    wanted = []
    for j in range(slots):
        gap = me - offset[j]
        peer = jnp.where(gap < 0, gap + device_count, gap)
        table[peer] = j
        stripe = peer * (slots // helpers) + j // helpers
        start = planes[0, stripe]
        wanted.append((start, planes[1, stripe] - start, planes[4, stripe] - start))
    for first in range(0, slots, TOGETHER):
        some = range(first, min(first + TOGETHER, slots))
        for j in some:
            loads[j].wait()
        for j in some:
            start, step, jump = wanted[j]
            mask = (col == start + jump * coarse + step * fine).astype(jnp.float32)
            rows = jnp.dot(mask.astype(held.dtype), held[j], preferred_element_type=jnp.float32)
            picked[j] = rows.astype(held.dtype)
    for out, receivers in zip(outs, rules):
        for k, receiver in enumerate(receivers):
            slot = table[receiver(me)]
            rows = jnp.where(slot >= 0, picked[jnp.maximum(slot, 0)], jnp.zeros((), held.dtype))
            out[pl.ds(k * plane_count, plane_count)] = rows


def pick_rows(rules, helpers, device_count, helper_offset, planes, store):
    slots, sub_total, columns = store.shape
    plane_count = planes.shape[0]
    counts = [len(r) * plane_count for r in rules]
    return pl.pallas_call(
        functools.partial(pick_kernel, rules, helpers),
        out_shape=[jax.ShapeDtypeStruct((count, columns), store.dtype) for count in counts],
        in_specs=[HBM] * 3,
        out_specs=[VMEM] * len(counts),
        scratch_shapes=[
            pltpu.VMEM((slots, sub_total, columns), store.dtype),
            pltpu.VMEM((slots, plane_count, columns), store.dtype),
            pltpu.SMEM(helper_offset.shape, jnp.int32),
            pltpu.SMEM(planes.shape, jnp.int32),
            pltpu.SMEM((device_count,), jnp.int32),
            pltpu.SemaphoreType.DMA((slots,)),
            pltpu.SemaphoreType.DMA((2,)),
        ],
        cost_estimate=pl.CostEstimate(
            flops=2 * slots * plane_count * sub_total * columns,
            bytes_accessed=2 * (slots * sub_total + sum(counts)) * columns,
            transcendentals=0,
        ),
        compiler_params=pltpu.CompilerParams(
            vmem_limit_bytes=2 * (slots * (sub_total + plane_count) + 2 * sum(counts)) * columns + (4 << 20)
        ),
        name="pick_rows",
    )(*(pltpu.with_memory_space_constraint(x, pltpu.HBM) for x in (helper_offset, planes, store)))


def put_kernel(rows_ref, out_ref, sems):
    size = rows_ref.shape[0] // sems.shape[0]
    parts = [pl.ds(i * size, size) for i in range(sems.shape[0])]
    copies = [pltpu.make_async_copy(rows_ref.at[p], out_ref.at[p], sems.at[i]) for i, p in enumerate(parts)]
    for copy in copies:
        copy.start()
    for copy in copies:
        copy.wait()


def put_in_hbm(rows):
    return pl.pallas_call(
        put_kernel,
        out_shape=jax.ShapeDtypeStruct(rows.shape, rows.dtype),
        in_specs=[VMEM],
        out_specs=HBM,
        scratch_shapes=[pltpu.SemaphoreType.DMA((4,))],
        cost_estimate=pl.CostEstimate(flops=0, bytes_accessed=4 * rows.size, transcendentals=0),
        compiler_params=pltpu.CompilerParams(vmem_limit_bytes=2 * rows.size + (4 << 20)),
        name="put_in_hbm",
    )(rows)


def gather_rows(scratch, rows_refs, counts):
    at = 0
    for r, count in zip(rows_refs, counts):
        scratch[pl.ds(at, count)] = r[pl.ds(0, count)]
        at += count


def add_terms(terms, out_rows):
    total = terms[:out_rows]
    for t in range(1, TERMS):
        total += terms[t * out_rows : (t + 1) * out_rows]
    return total


def begin_kernel(counts, matrix_ref, *refs):
    rows_refs, (out_ref, rows) = refs[: len(counts)], refs[len(counts) :]
    gather_rows(rows, rows_refs, counts)
    terms = jnp.dot(matrix_ref[:, : rows.shape[0]], rows[...], preferred_element_type=jnp.float32)
    out_ref[...] = add_terms(terms, out_ref.shape[0])


def finish_kernel(counts, skip, matrix_ref, begun_ref, *refs):
    rows_refs, (out_ref, made, rows, store_sem) = refs[: len(counts)], refs[len(counts) :]
    out_rows, columns = out_ref.shape
    gather_rows(rows, rows_refs, counts)
    wide = columns // PARTS
    stores = []
    for c in range(PARTS):
        part = pl.ds(c * wide, wide)
        total = begun_ref[:, part]
        if counts:
            terms = jnp.dot(matrix_ref[:, skip:], rows[:, part], preferred_element_type=jnp.float32)
            total += add_terms(terms, out_rows)
        made[:, part] = total.astype(made.dtype)
        stores.append(pltpu.make_async_copy(made.at[:, part], out_ref.at[:, part], store_sem.at[c]))
        stores[-1].start()
    for copy in stores:
        copy.wait()


def rebuild(matrix, pieces, counts, split):
    out_rows = matrix.shape[0] // TERMS
    columns = pieces[0].shape[1]
    early, late = sum(counts[:split]), sum(counts[split:])

    def settings(rows):
        return dict(
            cost_estimate=pl.CostEstimate(
                flops=2 * TERMS * out_rows * rows * columns,
                bytes_accessed=2 * columns * (rows + out_rows),
                transcendentals=0,
            ),
            compiler_params=pltpu.CompilerParams(
                vmem_limit_bytes=(4 * rows + 16 * out_rows) * columns + 4 * matrix.size + (4 << 20)
            ),
        )

    begun = pl.pallas_call(
        functools.partial(begin_kernel, counts[:split]),
        out_shape=jax.ShapeDtypeStruct((out_rows, columns), jnp.float32),
        in_specs=[VMEM] * (1 + split),
        out_specs=VMEM,
        scratch_shapes=[pltpu.VMEM((early, columns), jnp.bfloat16)],
        name="begin",
        **settings(early),
    )(matrix, *pieces[:split])
    return pl.pallas_call(
        functools.partial(finish_kernel, counts[split:], early),
        out_shape=jax.ShapeDtypeStruct((out_rows, columns), jnp.bfloat16),
        in_specs=[VMEM] * (2 + len(pieces) - split),
        out_specs=HBM,
        scratch_shapes=[
            pltpu.VMEM((out_rows, columns), jnp.bfloat16),
            pltpu.VMEM((max(late, 16), columns), jnp.bfloat16),
            pltpu.SemaphoreType.DMA((PARTS,)),
        ],
        name="finish",
        **settings(late),
    )(matrix, begun, *pieces[split:])


def in_terms(x):
    terms = []
    for _ in range(TERMS):
        terms.append(lax.reduce_precision(x, 8, 7))
        x = x - terms[-1]
    return jnp.concatenate(terms, 0).astype(jnp.bfloat16)


def repair_matrix(decode_block, pair_block, recouple_pairs, sources, peers):
    stripes_here, helpers, plane_count = pair_block.shape
    group_size = decode_block.shape[1]
    helper_ids = jnp.arange(helpers, dtype=jnp.int32)
    choose = (pair_block[..., None] == helper_ids).astype(jnp.float32)
    coupled = (pair_block != helper_ids[None, :, None]).astype(jnp.float32)
    unmix = (jnp.eye(helpers, dtype=jnp.float32)[None, :, None, :] - COUPLING * coupled[..., None] * choose) / (
        1.0 - COUPLING * COUPLING
    )
    sectioned = jnp.einsum("sth,shzg->sztg", decode_block, unmix, precision=HIGHEST)
    sub_count = plane_count * group_size
    rows_in = jnp.arange(peers.shape[0] * plane_count, dtype=jnp.int32)
    peer_of_row = jnp.repeat(peers, plane_count)
    at_row = (sources.reshape(stripes_here, helpers)[..., None] == peer_of_row).astype(jnp.float32)
    spread = jnp.einsum(
        "sag,sgr->sar", sectioned.reshape(stripes_here, sub_count, helpers), at_row, precision=HIGHEST
    )
    same_plane = jnp.arange(sub_count, dtype=jnp.int32)[:, None] // group_size == rows_in[None, :] % plane_count
    spread = jnp.where(same_plane[None], spread, 0.0)
    sub_ids = jnp.arange(sub_count, dtype=jnp.int32)
    pick = (recouple_pairs[..., None] == sub_ids).astype(jnp.float32)
    distinct = (recouple_pairs != sub_ids[None, :]).astype(jnp.float32)
    mixing = jnp.eye(sub_count, dtype=jnp.float32)[None] + COUPLING * distinct[..., None] * pick
    whole = jnp.einsum("sab,sbc->sac", mixing, spread, precision=HIGHEST)
    return whole.reshape(stripes_here * sub_count, peers.shape[0] * plane_count)


def swap(x, mask, device_count):
    return lax.ppermute(x, AXES, [(q, q ^ mask) for q in range(device_count)])


def body(span_store, helper_offset, plane_index, coupling_pair, decode_matrix, recouple_pair):
    rack_count, dev_count = lax.axis_size("rack"), lax.axis_size("dev")
    device_count = rack_count * dev_count
    me = lax.axis_index("rack") * dev_count + lax.axis_index("dev")
    columns = span_store.shape[-1]
    stripes_here, helpers, plane_count = coupling_pair.shape
    sub_count = recouple_pair.shape[1]
    near = near_masks(rack_count)
    ahead = ahead_chips(rack_count, dev_count)
    rules = outgoing_rules(near, ahead, rack_count, dev_count)
    outgoing = pick_rows(rules, helpers, device_count, helper_offset, plane_index.T, span_store)
    across = [swap(x, m * dev_count, device_count) for m, x in zip(near, outgoing)]
    groups = None
    if rack_count > 1:
        groups = [
            [rack * dev_count + d for d in range(dev_count) for rack in (r, rack_count - 1 - r)]
            for r in range(rack_count // 2)
        ]
    blocks = put_in_hbm(outgoing[-1]).reshape(-1, plane_count, columns)
    far = lax.all_to_all(blocks, AXES, 0, 0, axis_index_groups=groups, tiled=True).reshape(-1, columns)
    peers = [far_peer(me, i, rack_count, dev_count) for i in range(far.shape[0] // plane_count)]
    arrived, counts = [far], [far.shape[0]]
    if near:
        chips = range(dev_count // 2)
        straight = [
            swap(x, near[0] * dev_count + 2 * chip, device_count)
            for chip, x in zip(ahead, outgoing[len(near) :])
        ]
        home = [(x, m * dev_count, 0) for m, x in zip(near, across)]
        home += [(x, near[0] * dev_count + 2 * chip, 0) for chip, x in zip(ahead, straight)]
        onward = [
            [(x, m * dev_count + 2 * chip, chip) for m, x in zip(near, across) if m != near[0] or chip not in ahead]
            for chip in chips[1:]
        ]

        def block(x, index):
            return x[index * plane_count : (index + 1) * plane_count]

        crossing = [block(x, 2 * chip + 1) for x, _, chip in home + sum(onward, [])]
        crossed = swap(jnp.concatenate(crossing, 0), 1, device_count)
        arrived += [x for x, _, _ in home] + [crossed]
        counts += [plane_count] * len(home) + [len(home) * plane_count]
        peers += [me ^ mask for _, mask, _ in home] + [me ^ mask ^ 1 for _, mask, _ in home]
        at = len(home) * plane_count
        for chip, some in zip(chips[1:], onward):
            size = len(some) * plane_count
            part = [block(x, 2 * chip) for x, _, _ in some] + [crossed[at : at + size]]
            arrived.append(swap(jnp.concatenate(part, 0), 2 * chip, device_count))
            counts.append(2 * size)
            peers += [me ^ mask ^ core for core in (0, 1) for _, mask, _ in some]
            at += size
    split = len(arrived) - (dev_count // 2 - 1 if near else 0)
    sources = (me + helper_offset) % device_count
    peers = jnp.stack([jnp.asarray(p, jnp.int32) for p in peers])
    whole = in_terms(repair_matrix(decode_matrix, coupling_pair, recouple_pair, sources, peers))
    return rebuild(whole, arrived, counts, split).reshape(stripes_here, sub_count, columns)


def solution(mesh):
    split = ("rack", "dev")
    placed = (
        P(split, None, None),
        P(),
        P(),
        P(split, None, None),
        P(split, None, None),
        P(split, None),
    )
    return jax.shard_map(body, mesh=mesh, in_specs=placed, out_specs=P(split, None, None), check_vma=False)
```
